32 devices in a mesh: gx: 8 (over z, x), gy: 4 (over y, core).
Axes of the slice: x: 2, y: 2, z: 4, core: 2. Of those that a mesh axis runs over, the one named last changes fastest.
Arguments:
- right_side: float32 [32, 256, 2048], P(None, 'gx', 'gy'), may hold values from -6 to 6
- absorb: float32 [256, 2048], P('gx', 'gy'), may hold values from 0.05 to 4
- tiles: float32 [2, 1024, 512], replicated, may hold values from -0.0078125 to 0.0078125
- tile_index: int32 [256, 4], P('gx', 'gy'), may hold values from 0 to 1
- tile_sign: int32 [256, 4], P('gx', 'gy'), may hold values from 0 to 1
Outputs:
- solution: float32 [32, 256, 2048], P(None, 'gx', 'gy')
- residual: float32 [32, 256, 2048], P(None, 'gx', 'gy')
- sketched_residual: float32 [32, 1024], P(None, ('gx', 'gy'))
The draws below stay inside these ranges and needn't reach their ends.
Inputs may be any that keep to these rules, and one draw needn't show every extreme that they name: `tile_index`: which of the 2 tiles a row of a column block uses. `tile_sign`: 1 stands for the sign +1, 0 for -1.
All inputs are finite; a program needn't handle non-finite values.
Results may differ from the reference program's by a relative error of at most 0.006.
Values sent between devices are 32-bit elements; how exact they have to be, the bound alone decides.
A program may use at most 64 MiB of HBM per device.

```python
import math
import jax
import jax.numpy as jnp
from jax import lax

RHS = 32
CY = 512
SKETCH = 1024
TILES = 2
NX = 256
NY = 2048
N_GY = 4


def place_ends(drawn, key, smallest, high):
    longest = drawn.shape.index(max(drawn.shape))
    spots = []
    for shift in (0, 1):
        where = [jax.random.randint(jax.random.fold_in(key, axis), (), 0, length) for axis, length in enumerate(drawn.shape)]
        where[longest] = (where[longest] + shift) % drawn.shape[longest]
        spots.append(tuple(where))
    return drawn.at[spots[0]].set(smallest).at[spots[1]].set(high)


def shard_levels(stream_key, dims, shards, least, top_value):
    def one(axis_at, parts):
        heights = jax.random.uniform(jax.random.fold_in(jax.random.fold_in(stream_key, 6), axis_at), (parts,), jnp.float32, least / len(shards), top_value / len(shards))
        return jnp.repeat(jnp.exp(heights), dims[axis_at] // parts).reshape((-1,) + (1,) * (len(dims) - axis_at - 1))

    gain = one(*shards[0])
    for cut in shards[1:]:
        gain = gain * one(*cut)
    return gain


def centred(rng, dims, spread, reach, cuts=(), kind=jnp.bfloat16):
    drawn = jax.random.normal(rng, dims, jnp.float32) * spread
    if len(cuts) > 0:
        drawn = shard_levels(rng, dims, cuts, -0.22, 0.18) * drawn
    return jnp.clip(drawn, min=-reach, max=reach).astype(kind)


def setup_inputs(seed: int = 0) -> dict:
    key_of = jax.random.split(jax.random.key(seed), 6)
    return {
        "right_side": centred(key_of[0], (RHS, NX, NY), 1.0, 6.0, ((1, 8), (2, 4)), jnp.float32),
        "absorb": jnp.clip(jnp.exp(math.log(4.0) - 4.3820266 * jax.random.uniform(key_of[1], (NX, NY), jnp.float32) ** shard_levels(key_of[1], (NX, NY), ((0, 8), (1, 4)), -0.2, 0.2)), 0.05, 4.0),
        "tiles": centred(key_of[2], (TILES, SKETCH, CY), (NX * NY) ** -0.5, 0.0078125, (), jnp.float32),
        "tile_index": place_ends(jax.random.randint(key_of[3], (NX, N_GY), 0, TILES), jax.random.fold_in(key_of[3], 1), 0, TILES - 1).astype(jnp.int32),
        "tile_sign": place_ends(jax.random.randint(key_of[4], (NX, N_GY), 0, 2), jax.random.fold_in(key_of[4], 1), 0, 1).astype(jnp.int32),
    }


axial_x = 1.0
axial_y = 0.2
shear_half = 0.15
ridge_share = 1e-05

def operate(padded, absorb):
    center = padded[..., 1:-1, 1:-1]
    east_side = padded[..., 1:-1, 2:]
    west_side = padded[..., 1:-1, :-2]
    north_side = padded[..., :-2, 1:-1]
    south_side = padded[..., 2:, 1:-1]
    upper_right = padded[..., :-2, 2:]
    upper_left = padded[..., :-2, :-2]
    lower_right = padded[..., 2:, 2:]
    lower_left = padded[..., 2:, :-2]
    diagonal_weight = 2.0 * axial_x + 2.0 * axial_y
    lapl = diagonal_weight * center - axial_x * (east_side + west_side) - axial_y * (north_side + south_side)
    lapl = lapl - shear_half * (upper_right + lower_left) + shear_half * (upper_left + lower_right)
    return (lapl + absorb * center) / (diagonal_weight + absorb)

def sketch_field(field, tiles, tile_index, tile_sign):
    blocks = field.reshape(field.shape[0], tile_index.shape[0], tile_index.shape[1], tiles.shape[2])
    which = jnp.arange(tiles.shape[0], dtype=jnp.int32)
    signed = (2 * tile_sign - 1).astype(jnp.float32)
    picker = (tile_index[..., None] == which).astype(jnp.float32) * signed[..., None]
    folded = jnp.einsum('rgk,qrgc->qkc', picker, blocks, precision=lax.Precision.HIGHEST)
    return jnp.einsum('ksc,qkc->qs', tiles, folded, precision=lax.Precision.HIGHEST)

def local_products(sketches):
    basis_sketch = sketches[1:]
    gram_matrix = jnp.einsum('iqs,jqs->ijq', basis_sketch, basis_sketch, precision=lax.Precision.HIGHEST)
    projected = jnp.einsum('iqs,qs->iq', basis_sketch, sketches[0], precision=lax.Precision.HIGHEST)
    return (gram_matrix, projected)

def coefficients(gram_matrix, projected):
    ridge_term = ridge_share * (gram_matrix[0, 0] + gram_matrix[1, 1] + gram_matrix[2, 2])
    first_pivot = jnp.sqrt(gram_matrix[0, 0] + ridge_term)
    lower_10 = gram_matrix[1, 0] / first_pivot
    lower_20 = gram_matrix[2, 0] / first_pivot
    second_pivot = jnp.sqrt(gram_matrix[1, 1] + ridge_term - lower_10 * lower_10)
    lower_21 = (gram_matrix[2, 1] - lower_20 * lower_10) / second_pivot
    third_pivot = jnp.sqrt(gram_matrix[2, 2] + ridge_term - lower_20 * lower_20 - lower_21 * lower_21)
    forward_0 = projected[0] / first_pivot
    forward_1 = (projected[1] - lower_10 * forward_0) / second_pivot
    forward_2 = (projected[2] - lower_20 * forward_0 - lower_21 * forward_1) / third_pivot
    coeff_2 = forward_2 / third_pivot
    coeff_1 = (forward_1 - lower_21 * coeff_2) / second_pivot
    coeff_0 = (forward_0 - lower_10 * coeff_1 - lower_20 * coeff_2) / first_pivot
    return jnp.stack([coeff_0, coeff_1, coeff_2])

def reference(right_side, absorb, tiles, tile_index, tile_sign):
    basis = [right_side]
    current = right_side
    for step in range(3):
        padded = jnp.pad(current, ((0, 0), (1, 1), (1, 1)))
        current = operate(padded, absorb)
        basis.append(current)
    sketches = jnp.stack([sketch_field(field, tiles, tile_index, tile_sign) for field in basis])
    gram_matrix, projected = local_products(sketches)
    coeff = coefficients(gram_matrix, projected)
    solution = coeff[0][:, None, None] * basis[0] + coeff[1][:, None, None] * basis[1] + coeff[2][:, None, None] * basis[2]
    residual = right_side - (coeff[0][:, None, None] * basis[1] + coeff[1][:, None, None] * basis[2] + coeff[2][:, None, None] * basis[3])
    sketched_residual = sketches[0] - jnp.einsum('jq,jqs->qs', coeff, sketches[1:], precision=lax.Precision.HIGHEST)
    return (solution, residual, sketched_residual)
```

```python
import functools

import jax
import jax.numpy as jnp
from jax import lax
from jax.experimental import pallas as pl
from jax.experimental.pallas import tpu as pltpu
from jax.sharding import PartitionSpec as P

MESH = pl.DeviceIdType.MESH
DIAG = 2.4
RIDGE = 1e-05
HALO = 3
FULL = lax.Precision.HIGHEST


def kernel(
    ngx, ngy, rows, cols, width,
    x_ref, ab_ref, tiles_ref, w_ref,
    sol_ref, res_ref, skr_ref,
    v0, v1, v2, v3, inv, tl, packs, got, abh, fold, sk, part1, mid, part2, gath, gath1, gath2,
    sol_b, res_b,
    in_sem, out_sem, row_send, row_recv, col_send, col_recv, ab_send, ab_recv,
    s1s, s1r, s2s, s2r, g1s, g1r, g2s, g2r,
):
    gx = lax.axis_index("gx")
    gy = lax.axis_index("gy")
    ext = rows + 2 * HALO
    wide = cols + 128

    x_copy = pltpu.make_async_copy(x_ref, v0.at[HALO:HALO + rows, 0:32, 0:cols], in_sem.at[0])
    x_copy.start()
    t_copy = pltpu.make_async_copy(tiles_ref, tl, in_sem.at[1])
    t_copy.start()

    barrier = pltpu.get_barrier_semaphore()
    for k in range(1, ngx):
        pl.semaphore_signal(barrier, inc=1, device_id=(lax.rem(gx + k, ngx), gy), device_id_type=MESH)
    for k in range(1, ngy):
        pl.semaphore_signal(barrier, inc=1, device_id=(gx, lax.rem(gy + k, ngy)), device_id_type=MESH)
    up, down = gx > 0, gx < ngx - 1
    left, right = gy > 0, gy < ngy - 1
    there = {-1: up, 0: None, 1: down}
    side_there = (left, right)

    def both(a, b):
        return b if a is None else jnp.logical_and(a, b)

    for dx in (-1, 1):
        for side, dy in enumerate((-1, 1)):
            @pl.when(both(there[dx], side_there[side]))
            def _(dx=dx, dy=dy):
                pl.semaphore_signal(barrier, inc=1, device_id=(gx + dx, gy + dy), device_id_type=MESH)
    n_v = up.astype(jnp.int32) + down.astype(jnp.int32)
    n_h = left.astype(jnp.int32) + right.astype(jnp.int32)

    for r in range(rows):
        v0[HALO + r, 32:40, 0:cols] = jnp.broadcast_to(ab_ref[r:r + 1, :], (8, cols))
    x_copy.wait()

    lane = lax.broadcasted_iota(jnp.int32, (40, 128), 1)

    def pack(r, acc):
        here = (lane >= 4 * r) & (lane < 4 * r + 4)
        first = pltpu.roll(v0[HALO + r, :, 0:128], 4 * r, 1)
        last = pltpu.roll(v0[HALO + r, :, cols - 128:cols], lax.rem(4 * r + 4, 128), 1)
        return jnp.where(here, first, acc[0]), jnp.where(here, last, acc[1])

    zero = jnp.zeros((40, 128), jnp.float32)
    first, last = lax.fori_loop(0, rows, pack, (zero, zero))
    packs[0] = first
    packs[1] = last

    pl.semaphore_wait(barrier, ngx - 1 + ngy - 1 + n_v * n_h)

    row_copies = []
    for d, (dx, here) in enumerate(((-1, up), (1, down))):
        src = HALO if dx < 0 else rows
        dst = HALO + rows if dx < 0 else 0
        row_copies.append((pltpu.make_async_remote_copy(
            src_ref=v0.at[src:src + HALO, 0:32, 0:cols], dst_ref=v0.at[dst:dst + HALO, 0:32, 0:cols],
            send_sem=row_send.at[d], recv_sem=row_recv.at[d],
            device_id=(gx + dx, gy), device_id_type=MESH), here, (down, up)[d]))
        ar = 0 if dx < 0 else rows - 8
        row_copies.append((pltpu.make_async_remote_copy(
            src_ref=ab_ref.at[ar:ar + 8, :], dst_ref=abh.at[d],
            send_sem=ab_send.at[d], recv_sem=ab_recv.at[d],
            device_id=(gx + dx, gy), device_id_type=MESH), here, (down, up)[d]))
    col_copies = []
    for side, dy in enumerate((-1, 1)):
        for i, dx in enumerate((0, -1, 1)):
            slot = side * 3 + i
            to = both(there[dx], side_there[side])
            frm = both(there[-dx], side_there[1 - side])
            col_copies.append((pltpu.make_async_remote_copy(
                src_ref=packs.at[side], dst_ref=got.at[slot],
                send_sem=col_send.at[slot], recv_sem=col_recv.at[slot],
                device_id=(gx + dx, gy + dy), device_id_type=MESH), to, frm))
    for copy, to, frm in col_copies + row_copies:
        @pl.when(to)
        def _(copy=copy):
            copy.start()

    for d, frm in enumerate((down, up)):
        dst = HALO + rows if d == 0 else 0
        @pl.when(jnp.logical_not(frm))
        def _(d=d, dst=dst):
            v0[dst:dst + HALO, 0:32, 0:cols] = jnp.zeros((HALO, 32, cols), jnp.float32)
            abh[d] = jnp.zeros((8, cols), jnp.float32)
    for slot, (copy, to, frm) in enumerate(col_copies):
        @pl.when(jnp.logical_not(frm))
        def _(slot=slot):
            got[slot] = jnp.zeros((40, 128), jnp.float32)

    for copy, to, frm in col_copies + row_copies:
        @pl.when(frm)
        def _(copy=copy):
            copy.wait_recv()

    for i in range(HALO):
        v0[i, 32:40, 0:cols] = jnp.broadcast_to(abh[1, 8 - HALO + i:8 - HALO + i + 1, :], (8, cols))
        v0[HALO + rows + i, 32:40, 0:cols] = jnp.broadcast_to(abh[0, i:i + 1, :], (8, cols))

    def unpack(slot_right, slot_left, r, dest):
        a = pltpu.roll(got[slot_right], lax.rem(128 - 4 * r, 128), 1)
        b = pltpu.roll(got[slot_left], lax.rem(252 - 4 * r, 128), 1)
        v0[dest, :, cols:wide] = jnp.where(lane < 4, a, jnp.where(lane >= 124, b, 0.0))

    def unpack_own(r, c):
        unpack(0, 3, r, HALO + r)
        return c

    lax.fori_loop(0, rows, unpack_own, 0)
    for i in range(HALO):
        unpack(1, 4, i, HALO + rows + i)
        unpack(2, 5, rows - HALO + i, i)

    lane_w = lax.broadcasted_iota(jnp.int32, (8, wide), 1)
    col_in = (lane_w < cols) | ((lane_w < cols + HALO) & right) | ((lane_w >= wide - HALO) & left)

    def make_inv(r, c):
        row = gx * rows + r - HALO
        ok = col_in & (row >= 0) & (row < rows * ngx)
        inv[r] = jnp.where(ok, 1.0 / (DIAG + v0[r, 32:40, :]), 0.0)
        return c

    lax.fori_loop(0, ext, make_inv, 0)

    def step(src, dst, n, lo, hi):
        for t in range(4):
            q = slice(8 * t, 8 * t + 8)

            def parts(r):
                v = src[r, q, :]
                e = pltpu.roll(v, wide - 1, 1)
                w = pltpu.roll(v, 1, 1)
                return v, e + w, e - w

            vp, _, dp = parts(lo - 1)
            up0 = 0.2 * vp + 0.15 * dp
            z = jnp.zeros((8, cols), jnp.float32)

            def body(r, carry):
                upv, v, s, d, a0, a1, b0, b1 = carry
                vn, sn, dn = parts(r + 1)
                out = v - inv[r] * (s + upv + (0.2 * vn - 0.15 * dn))
                dst[r, q, :] = out
                o = out[:, 0:cols]
                a0 = a0 + w_ref[0, r] * o
                a1 = a1 + w_ref[1, r] * o
                if n == 1:
                    b0 = b0 + w_ref[0, r] * v[:, 0:cols]
                    b1 = b1 + w_ref[1, r] * v[:, 0:cols]
                return 0.2 * v + 0.15 * d, vn, sn, dn, a0, a1, b0, b1

            v, s, d = parts(lo)
            _, _, _, _, a0, a1, b0, b1 = lax.fori_loop(lo, hi, body, (up0, v, s, d, z, z, z, z))
            fold[0, 32 * n + 8 * t:32 * n + 8 * t + 8, :] = a0
            fold[1, 32 * n + 8 * t:32 * n + 8 * t + 8, :] = a1
            if n == 1:
                fold[0, q, :] = b0
                fold[1, q, :] = b1

    step(v0, v1, 1, 1, ext - 1)
    step(v1, v2, 2, 2, ext - 2)
    step(v2, v3, 3, 3, ext - 3)
    t_copy.wait()

    block = ngy * width

    def mm(g, c):
        rows_g = pl.ds(pl.multiple_of(g * block, block), block)
        out = jnp.zeros((block, 128), jnp.float32)
        for k in range(2):
            out = out + lax.dot_general(
                tl[k, rows_g, :], fold[k], (((1,), (1,)), ((), ())),
                precision=FULL, preferred_element_type=jnp.float32)
        for j in range(ngy):
            sk[j, g] = out[j * width:(j + 1) * width, :]
        return c

    lax.fori_loop(0, ngx, mm, 0)

    def exchange(n, axis, pick, land, ss, rs):
        me = gx if axis == 0 else gy
        out = []
        for k in range(1, n):
            peer = lax.rem(me + k, n)
            out.append(pltpu.make_async_remote_copy(
                src_ref=pick(peer), dst_ref=land.at[k - 1], send_sem=ss.at[k - 1], recv_sem=rs.at[k - 1],
                device_id=(peer, gy) if axis == 0 else (gx, peer), device_id_type=MESH))
        for c in out:
            c.start()
        return out

    c1 = exchange(ngy, 1, lambda p: sk.at[p], part1, s1s, s1r)
    total = sk[gy]
    for k, c in enumerate(c1):
        c.wait_recv()
        total = total + part1[k]
    mid[...] = total
    c2 = exchange(ngx, 0, lambda p: mid.at[p], part2, s2s, s2r)
    own = mid[gx]
    for k, c in enumerate(c2):
        c.wait_recv()
        own = own + part2[k]

    prods = [jnp.sum(own * own, 0, keepdims=True)]
    for k in (1, 2):
        prods.append(jnp.sum(own * pltpu.roll(own, 32 * k, 1), 0, keepdims=True))
    gath[0] = jnp.concatenate(prods + [jnp.zeros((5, 128), jnp.float32)], 0)
    c3 = exchange(ngy, 1, lambda p: gath.at[0], gath1, g1s, g1r)
    tot = gath[0]
    for k, c in enumerate(c3):
        c.wait_recv()
        tot = tot + gath1[k]
    gath[1] = tot
    c4 = exchange(ngx, 0, lambda p: gath.at[1], gath2, g2s, g2r)
    for k, c in enumerate(c4):
        c.wait_recv()
        tot = tot + gath2[k]

    by = [tot] + [pltpu.roll(tot, 128 - 32 * f, 1) for f in (1, 2, 3)]

    def at(k, f):
        return by[f][k:k + 1, :]

    g00, g11, g22 = at(0, 1), at(0, 2), at(0, 3)
    g10, g21, g20 = at(1, 2), at(1, 3), at(2, 3)
    h0, h1, h2 = at(1, 1), at(2, 2), at(1, 0)
    ridge = RIDGE * (g00 + g11 + g22)
    p0 = jnp.sqrt(g00 + ridge)
    l10 = g10 / p0
    l20 = g20 / p0
    p1 = jnp.sqrt(g11 + ridge - l10 * l10)
    l21 = (g21 - l20 * l10) / p1
    p2 = jnp.sqrt(g22 + ridge - l20 * l20 - l21 * l21)
    f0 = h0 / p0
    f1 = (h1 - l10 * f0) / p1
    f2 = (h2 - l20 * f0 - l21 * f1) / p2
    y2 = f2 / p2
    y1 = (f1 - l21 * y2) / p1
    y0 = (f0 - l10 * y1 - l20 * y2) / p0

    skr_ref[...] = own - (y0 * pltpu.roll(own, 96, 1) + y1 * pltpu.roll(own, 64, 1) + y2 * pltpu.roll(own, 32, 1))

    same = lax.broadcasted_iota(jnp.int32, (32, 128), 0) == lax.broadcasted_iota(jnp.int32, (32, 128), 1)
    c0, c1_, c2_ = [
        jnp.sum(jnp.where(same, jnp.broadcast_to(y, (32, 128)), 0.0), 1, keepdims=True) for y in (y0, y1, y2)
    ]

    n_out = 4
    each = rows // n_out
    outs = []
    for b in range(n_out):
        def combine(r, c, b=b):
            for t in range(4):
                q = slice(8 * t, 8 * t + 8)
                k0, k1, k2 = c0[q], c1_[q], c2_[q]
                a, bb, cc, dd = [v[HALO + r, q, 0:cols] for v in (v0, v1, v2, v3)]
                sol_b[r, q, :] = k0 * a + k1 * bb + k2 * cc
                res_b[r, q, :] = a - (k0 * bb + k1 * cc + k2 * dd)
            return c

        lax.fori_loop(b * each, (b + 1) * each, combine, 0)
        for o, (buf, ref) in enumerate(((sol_b, sol_ref), (res_b, res_ref))):
            part = slice(b * each, (b + 1) * each)
            oc = pltpu.make_async_copy(buf.at[part], ref.at[part], out_sem.at[2 * b + o])
            oc.start()
            outs.append(oc)

    for copy, to, frm in col_copies + row_copies:
        @pl.when(to)
        def _(copy=copy):
            copy.wait_send()
    for c in c1 + c2 + c3 + c4:
        c.wait_send()
    for oc in outs:
        oc.wait()


def shards(ngx, ngy, right_side, absorb, tiles, tile_index, tile_sign):
    count, rows, cols = right_side.shape
    sketch = tiles.shape[1]
    width = sketch // (ngx * ngy)
    ext, wide = rows + 2 * HALO, cols + 128
    which = jnp.arange(tiles.shape[0], dtype=jnp.int32)[:, None]
    weights = jnp.where(tile_index[:, 0][None] == which, (2 * tile_sign[:, 0] - 1)[None], 0).astype(jnp.float32)
    weights = jnp.pad(weights, ((0, 0), (HALO, HALO)))
    f32 = jnp.float32
    dma = pltpu.SemaphoreType.DMA
    any_spec = pl.BlockSpec(memory_space=pl.ANY)
    vmem_spec = pl.BlockSpec(memory_space=pltpu.VMEM)
    sol, res, skr = pl.pallas_call(
        functools.partial(kernel, ngx, ngy, rows, cols, width),
        out_shape=(
            jax.ShapeDtypeStruct((rows, count, cols), f32),
            jax.ShapeDtypeStruct((rows, count, cols), f32),
            jax.ShapeDtypeStruct((width, 128), f32),
        ),
        in_specs=[any_spec, vmem_spec, any_spec, pl.BlockSpec(memory_space=pltpu.SMEM)],
        out_specs=(any_spec, any_spec, vmem_spec),
        scratch_shapes=[
            pltpu.VMEM((ext, 40, wide), f32),
            pltpu.VMEM((ext, 32, wide), f32),
            pltpu.VMEM((ext, 32, wide), f32),
            pltpu.VMEM((ext, 32, wide), f32),
            pltpu.VMEM((ext, 8, wide), f32),
            pltpu.VMEM(tiles.shape, f32),
            pltpu.VMEM((2, 40, 128), f32),
            pltpu.VMEM((6, 40, 128), f32),
            pltpu.VMEM((2, 8, cols), f32),
            pltpu.VMEM((2, 128, cols), f32),
            pltpu.VMEM((ngy, ngx, width, 128), f32),
            pltpu.VMEM((ngy - 1, ngx, width, 128), f32),
            pltpu.VMEM((ngx, width, 128), f32),
            pltpu.VMEM((ngx - 1, width, 128), f32),
            pltpu.VMEM((2, 8, 128), f32),
            pltpu.VMEM((ngy - 1, 8, 128), f32),
            pltpu.VMEM((ngx - 1, 8, 128), f32),
            pltpu.VMEM((rows, count, cols), f32),
            pltpu.VMEM((rows, count, cols), f32),
            dma((2,)), dma((8,)), dma((2,)), dma((2,)), dma((6,)), dma((6,)), dma((2,)), dma((2,)),
            dma((ngy - 1,)), dma((ngy - 1,)), dma((ngx - 1,)), dma((ngx - 1,)),
            dma((ngy - 1,)), dma((ngy - 1,)), dma((ngx - 1,)), dma((ngx - 1,)),
        ],
        compiler_params=pltpu.CompilerParams(
            collective_id=0, has_side_effects=True, vmem_limit_bytes=56 * 2**20
        ),
    )(jnp.transpose(right_side, (1, 0, 2)), absorb, tiles, weights)
    return jnp.transpose(sol, (1, 0, 2)), jnp.transpose(res, (1, 0, 2)), skr[:, :count].T


def solution(mesh):
    in_specs = (P(None, "gx", "gy"), P("gx", "gy"), P(), P("gx", "gy"), P("gx", "gy"))
    out_specs = (P(None, "gx", "gy"), P(None, "gx", "gy"), P(None, ("gx", "gy")))
    fn = functools.partial(shards, mesh.shape["gx"], mesh.shape["gy"])
    return jax.shard_map(fn, mesh=mesh, in_specs=in_specs, out_specs=out_specs, check_vma=False)
```

```python
import functools

import jax
import jax.numpy as jnp
from jax import lax
from jax.experimental import pallas as pl
from jax.experimental.pallas import tpu as pltpu
from jax.sharding import PartitionSpec as P

MESH = pl.DeviceIdType.MESH
DIAG = 2.4
RIDGE = 1e-05
HALO = 3
UNROLL = 14


def kernel(
    ngx, ngy, rows, cols, width,
    x_ref, ab_ref, tiles_ref, index_ref, sign_ref,
    basis_ref, y_ref, skr_ref,
    v0, v1, v2, v3, inv, tl, packs, got, abh, fold, sk, part1, mid, part2, gath, gath1, gath2,
    w_ref,
    in_sem, out_sem, row_send, row_recv, col_send, col_recv, ab_send, ab_recv,
    s1s, s1r, s2s, s2r, g1s, g1r, g2s, g2r,
):
    gx = lax.axis_index("gx")
    gy = lax.axis_index("gy")
    ext = rows + 2 * HALO
    wide = cols + 128

    x_copy = pltpu.make_async_copy(x_ref, v0.at[HALO:HALO + rows, 0:32, 0:cols], in_sem.at[0])
    for r in range(rows):
        pltpu.make_async_copy(x_ref.at[:, r, :], v0.at[HALO + r, 0:32, 0:cols], in_sem.at[0]).start()
    t_copy = pltpu.make_async_copy(tiles_ref, tl, in_sem.at[1])
    t_copy.start()

    barrier = pltpu.get_barrier_semaphore()
    for k in range(1, ngx):
        pl.semaphore_signal(barrier, inc=1, device_id=(lax.rem(gx + k, ngx), gy), device_id_type=MESH)
    for k in range(1, ngy):
        pl.semaphore_signal(barrier, inc=1, device_id=(gx, lax.rem(gy + k, ngy)), device_id_type=MESH)
    up, down = gx > 0, gx < ngx - 1
    left, right = gy > 0, gy < ngy - 1
    there = {-1: up, 0: None, 1: down}
    side_there = (left, right)

    def both(a, b):
        return b if a is None else jnp.logical_and(a, b)

    for dx in (-1, 1):
        for side, dy in enumerate((-1, 1)):
            @pl.when(both(there[dx], side_there[side]))
            def _(dx=dx, dy=dy):
                pl.semaphore_signal(barrier, inc=1, device_id=(gx + dx, gy + dy), device_id_type=MESH)
    n_v = up.astype(jnp.int32) + down.astype(jnp.int32)
    n_h = left.astype(jnp.int32) + right.astype(jnp.int32)

    for r in range(ext):
        if HALO <= r < HALO + rows:
            sign = (2 * sign_ref[r - HALO] - 1).astype(jnp.float32)
            for k in range(2):
                w_ref[k, r] = jnp.where(index_ref[r - HALO] == k, sign, 0.0)
        else:
            w_ref[0, r] = 0.0
            w_ref[1, r] = 0.0

    for r in range(rows):
        v0[HALO + r, 32:40, 0:cols] = jnp.broadcast_to(ab_ref[r:r + 1, :], (8, cols))
    x_copy.wait()

    lane = lax.broadcasted_iota(jnp.int32, (40, 128), 1)

    def pack(r, acc):
        here = (lane >= 4 * r) & (lane < 4 * r + 4)
        first = pltpu.roll(v0[HALO + r, :, 0:128], 4 * r, 1)
        last = pltpu.roll(v0[HALO + r, :, cols - 128:cols], lax.rem(4 * r + 4, 128), 1)
        return jnp.where(here, first, acc[0]), jnp.where(here, last, acc[1])

    zero = jnp.zeros((40, 128), jnp.float32)
    first, last = lax.fori_loop(0, rows, pack, (zero, zero))
    packs[0] = first
    packs[1] = last

    pl.semaphore_wait(barrier, ngx - 1 + ngy - 1 + n_v * n_h)

    row_copies = []
    for d, (dx, here) in enumerate(((-1, up), (1, down))):
        src = HALO if dx < 0 else rows
        dst = HALO + rows if dx < 0 else 0
        row_copies.append((pltpu.make_async_remote_copy(
            src_ref=v0.at[src:src + HALO, 0:32, 0:cols], dst_ref=v0.at[dst:dst + HALO, 0:32, 0:cols],
            send_sem=row_send.at[d], recv_sem=row_recv.at[d],
            device_id=(gx + dx, gy), device_id_type=MESH), here, (down, up)[d]))
        ar = 0 if dx < 0 else rows - 8
        row_copies.append((pltpu.make_async_remote_copy(
            src_ref=ab_ref.at[ar:ar + 8, :], dst_ref=abh.at[d],
            send_sem=ab_send.at[d], recv_sem=ab_recv.at[d],
            device_id=(gx + dx, gy), device_id_type=MESH), here, (down, up)[d]))
    col_copies = []
    for side, dy in enumerate((-1, 1)):
        for i, dx in enumerate((0, -1, 1)):
            slot = side * 3 + i
            to = both(there[dx], side_there[side])
            frm = both(there[-dx], side_there[1 - side])
            col_copies.append((pltpu.make_async_remote_copy(
                src_ref=packs.at[side], dst_ref=got.at[slot],
                send_sem=col_send.at[slot], recv_sem=col_recv.at[slot],
                device_id=(gx + dx, gy + dy), device_id_type=MESH), to, frm))
    for copy, to, frm in col_copies + row_copies:
        @pl.when(to)
        def _(copy=copy):
            copy.start()

    for d, frm in enumerate((down, up)):
        dst = HALO + rows if d == 0 else 0
        @pl.when(jnp.logical_not(frm))
        def _(d=d, dst=dst):
            v0[dst:dst + HALO, 0:32, 0:cols] = jnp.zeros((HALO, 32, cols), jnp.float32)
            abh[d] = jnp.zeros((8, cols), jnp.float32)
    for slot, (copy, to, frm) in enumerate(col_copies):
        @pl.when(jnp.logical_not(frm))
        def _(slot=slot):
            got[slot] = jnp.zeros((40, 128), jnp.float32)

    z = jnp.zeros((8, cols), jnp.float32)
    for t in range(4):
        q0 = slice(8 * t, 8 * t + 8)

        def fold_rows(r, acc, q0=q0):
            a0, a1 = acc
            for u in range(4):
                o = v0[r * 4 + u + HALO, q0, 0:cols]
                a0 = a0 + w_ref[0, r * 4 + u + HALO] * o
                a1 = a1 + w_ref[1, r * 4 + u + HALO] * o
            return a0, a1

        a0, a1 = lax.fori_loop(0, rows // 4, fold_rows, (z, z))
        fold[0, q0, :] = a0
        fold[1, q0, :] = a1

    def wait_recv(copies):
        for copy, to, frm in copies:
            @pl.when(frm)
            def _(copy=copy):
                copy.wait_recv()

    wait_recv([col_copies[0], col_copies[3]])

    def unpack(slot_right, slot_left, r, dest):
        a = pltpu.roll(got[slot_right], lax.rem(128 - 4 * r, 128), 1)
        b = pltpu.roll(got[slot_left], lax.rem(252 - 4 * r, 128), 1)
        v0[dest, :, cols:wide] = jnp.where(lane < 4, a, jnp.where(lane >= 124, b, 0.0))

    lane_w = lax.broadcasted_iota(jnp.int32, (8, wide), 1)
    col_in = (lane_w < cols) | ((lane_w < cols + HALO) & right) | ((lane_w >= wide - HALO) & left)

    def make_inv(r):
        row = gx * rows + r - HALO
        ok = col_in & (row >= 0) & (row < rows * ngx)
        inv[r] = jnp.where(ok, 1.0 / (DIAG + v0[r, 32:40, :]), 0.0)

    def unpack_own(r, c):
        for u in range(4):
            unpack(0, 3, 4 * r + u, HALO + 4 * r + u)
        for u in range(4):
            make_inv(HALO + 4 * r + u)
        return c

    lax.fori_loop(0, rows // 4, unpack_own, 0)

    def step(src, dst, n, lo, hi, unroll, fresh):
        for t in range(4):
            q = slice(8 * t, 8 * t + 8)

            def parts(r):
                v = src[r, q, :]
                e = pltpu.roll(v, wide - 1, 1)
                w = pltpu.roll(v, 1, 1)
                return v, e + w, e - w

            vp, _, dp = parts(lo - 1)
            up0 = 0.2 * vp + 0.15 * dp

            def row(r, carry):
                upv, v, s, d, a0, a1 = carry
                vn, sn, dn = parts(r + 1)
                out = v - inv[r] * (s + upv + (0.2 * vn - 0.15 * dn))
                dst[r, q, :] = out
                o = out[:, 0:cols]
                a0 = a0 + w_ref[0, r] * o
                a1 = a1 + w_ref[1, r] * o
                return 0.2 * v + 0.15 * d, vn, sn, dn, a0, a1

            def body(i, carry):
                for u in range(unroll):
                    carry = row(lo + i * unroll + u, carry)
                return carry

            v, s, d = parts(lo)
            fq = slice(32 * n + 8 * t, 32 * n + 8 * t + 8)
            start = (z, z) if fresh else (fold[0, fq, :], fold[1, fq, :])
            carry = (up0, v, s, d) + start
            trips = (hi - lo) // unroll
            if trips > 1:
                carry = lax.fori_loop(0, trips, body, carry)
            else:
                carry = body(0, carry)
            for r in range(lo + trips * unroll, hi):
                carry = row(r, carry)
            fold[0, fq, :] = carry[4]
            fold[1, fq, :] = carry[5]

    for n, (src, dst) in enumerate(((v0, v1), (v1, v2), (v2, v3)), 1):
        step(src, dst, n, HALO + n, ext - HALO - n, UNROLL, True)

    wait_recv(col_copies[1:3] + col_copies[4:] + row_copies)
    for i in range(HALO):
        v0[i, 32:40, 0:cols] = jnp.broadcast_to(abh[1, 8 - HALO + i:8 - HALO + i + 1, :], (8, cols))
        v0[HALO + rows + i, 32:40, 0:cols] = jnp.broadcast_to(abh[0, i:i + 1, :], (8, cols))
        unpack(1, 4, i, HALO + rows + i)
        unpack(2, 5, rows - HALO + i, i)
    for i in range(HALO):
        make_inv(i)
        make_inv(HALO + rows + i)
    for n, (src, dst) in enumerate(((v0, v1), (v1, v2), (v2, v3)), 1):
        step(src, dst, n, n, HALO + n, HALO, False)
        step(src, dst, n, ext - HALO - n, ext - n, HALO, False)
    out_copies = []
    for n, v in enumerate((v1, v2, v3)):
        for r in range(rows):
            pltpu.make_async_copy(v.at[HALO + r, :, 0:cols], basis_ref.at[n, :, r, :], out_sem.at[n]).start()
        out_copies.append(pltpu.make_async_copy(v.at[HALO:HALO + rows, :, 0:cols], basis_ref.at[n], out_sem.at[n]))
    t_copy.wait()

    block = ngy * width

    def halves(a):
        hi = a.astype(jnp.bfloat16)
        return hi, (a - hi.astype(jnp.float32)).astype(jnp.bfloat16)

    fold_hi, fold_lo = zip(*[halves(fold[k]) for k in range(2)])

    def nt(a, b):
        return lax.dot_general(a, b, (((1,), (1,)), ((), ())), preferred_element_type=jnp.float32)

    def mm(g, c):
        rows_g = pl.ds(pl.multiple_of(g * block, block), block)
        out = jnp.zeros((block, 128), jnp.float32)
        for k in range(2):
            hi, lo = halves(tl[k, rows_g, :])
            out = out + (nt(hi, fold_hi[k]) + (nt(hi, fold_lo[k]) + nt(lo, fold_hi[k])))
        for j in range(ngy):
            sk[j, g] = out[j * width:(j + 1) * width, :]
        return c

    lax.fori_loop(0, ngx, mm, 0)

    def exchange(n, axis, pick, land, ss, rs):
        me = gx if axis == 0 else gy
        out = []
        for k in range(1, n):
            peer = lax.rem(me + k, n)
            out.append(pltpu.make_async_remote_copy(
                src_ref=pick(peer), dst_ref=land.at[k - 1], send_sem=ss.at[k - 1], recv_sem=rs.at[k - 1],
                device_id=(peer, gy) if axis == 0 else (gx, peer), device_id_type=MESH))
        for c in out:
            c.start()
        return out

    c1 = exchange(ngy, 1, lambda p: sk.at[p], part1, s1s, s1r)
    total = sk[gy]
    for k, c in enumerate(c1):
        c.wait_recv()
        total = total + part1[k]
    mid[...] = total
    c2 = exchange(ngx, 0, lambda p: mid.at[p], part2, s2s, s2r)
    own = mid[gx]
    for k, c in enumerate(c2):
        c.wait_recv()
        own = own + part2[k]

    prods = [jnp.sum(own * own, 0, keepdims=True)]
    for k in (1, 2):
        prods.append(jnp.sum(own * pltpu.roll(own, 32 * k, 1), 0, keepdims=True))
    gath[0] = jnp.concatenate(prods + [jnp.zeros((5, 128), jnp.float32)], 0)
    c3 = exchange(ngy, 1, lambda p: gath.at[0], gath1, g1s, g1r)
    tot = gath[0]
    for k, c in enumerate(c3):
        c.wait_recv()
        tot = tot + gath1[k]
    gath[1] = tot
    c4 = exchange(ngx, 0, lambda p: gath.at[1], gath2, g2s, g2r)
    for k, c in enumerate(c4):
        c.wait_recv()
        tot = tot + gath2[k]

    by = [tot] + [pltpu.roll(tot, 128 - 32 * f, 1) for f in (1, 2, 3)]

    def at(k, f):
        return by[f][k:k + 1, :]

    g00, g11, g22 = at(0, 1), at(0, 2), at(0, 3)
    g10, g21, g20 = at(1, 2), at(1, 3), at(2, 3)
    h0, h1, h2 = at(1, 1), at(2, 2), at(1, 0)
    ridge = RIDGE * (g00 + g11 + g22)
    p0 = jnp.sqrt(g00 + ridge)
    l10 = g10 / p0
    l20 = g20 / p0
    p1 = jnp.sqrt(g11 + ridge - l10 * l10)
    l21 = (g21 - l20 * l10) / p1
    p2 = jnp.sqrt(g22 + ridge - l20 * l20 - l21 * l21)
    f0 = h0 / p0
    f1 = (h1 - l10 * f0) / p1
    f2 = (h2 - l20 * f0 - l21 * f1) / p2
    y2 = f2 / p2
    y1 = (f1 - l21 * y2) / p1
    y0 = (f0 - l10 * y1 - l20 * y2) / p0

    skr_ref[...] = own - (y0 * pltpu.roll(own, 96, 1) + y1 * pltpu.roll(own, 64, 1) + y2 * pltpu.roll(own, 32, 1))

    y_ref[...] = jnp.concatenate([y0, y1, y2, jnp.zeros((5, 128), jnp.float32)], 0)

    for copy, to, frm in col_copies + row_copies:
        @pl.when(to)
        def _(copy=copy):
            copy.wait_send()
    for c in c1 + c2 + c3 + c4:
        c.wait_send()
    for oc in out_copies:
        oc.wait()


def shards(ngx, ngy, right_side, absorb, tiles, tile_index, tile_sign):
    count, rows, cols = right_side.shape
    sketch = tiles.shape[1]
    width = sketch // (ngx * ngy)
    ext, wide = rows + 2 * HALO, cols + 128
    f32 = jnp.float32
    dma = pltpu.SemaphoreType.DMA
    any_spec = pl.BlockSpec(memory_space=pl.ANY)
    vmem_spec = pl.BlockSpec(memory_space=pltpu.VMEM)
    basis, y, skr = pl.pallas_call(
        functools.partial(kernel, ngx, ngy, rows, cols, width),
        out_shape=(
            jax.ShapeDtypeStruct((3, count, rows, cols), f32),
            jax.ShapeDtypeStruct((8, 128), f32),
            jax.ShapeDtypeStruct((width, 128), f32),
        ),
        in_specs=[any_spec, vmem_spec, any_spec] + [pl.BlockSpec(memory_space=pltpu.SMEM)] * 2,
        out_specs=(any_spec, vmem_spec, vmem_spec),
        scratch_shapes=[
            pltpu.VMEM((ext, 40, wide), f32),
            pltpu.VMEM((ext, 32, wide), f32),
            pltpu.VMEM((ext, 32, wide), f32),
            pltpu.VMEM((ext, 32, wide), f32),
            pltpu.VMEM((ext, 8, wide), f32),
            pltpu.VMEM(tiles.shape, f32),
            pltpu.VMEM((2, 40, 128), f32),
            pltpu.VMEM((6, 40, 128), f32),
            pltpu.VMEM((2, 8, cols), f32),
            pltpu.VMEM((2, 128, cols), f32),
            pltpu.VMEM((ngy, ngx, width, 128), f32),
            pltpu.VMEM((ngy - 1, ngx, width, 128), f32),
            pltpu.VMEM((ngx, width, 128), f32),
            pltpu.VMEM((ngx - 1, width, 128), f32),
            pltpu.VMEM((2, 8, 128), f32),
            pltpu.VMEM((ngy - 1, 8, 128), f32),
            pltpu.VMEM((ngx - 1, 8, 128), f32),
            pltpu.SMEM((2, ext), f32),
            dma((2,)), dma((3,)), dma((2,)), dma((2,)), dma((6,)), dma((6,)), dma((2,)), dma((2,)),
            dma((ngy - 1,)), dma((ngy - 1,)), dma((ngx - 1,)), dma((ngx - 1,)),
            dma((ngy - 1,)), dma((ngy - 1,)), dma((ngx - 1,)), dma((ngx - 1,)),
        ],
        compiler_params=pltpu.CompilerParams(
            collective_id=0, has_side_effects=True, vmem_limit_bytes=56 * 2**20
        ),
    )(right_side, absorb, tiles, tile_index[:, 0], tile_sign[:, 0])
    c0, c1, c2 = [y[k, :count, None, None] for k in range(3)]
    solved = c0 * right_side + c1 * basis[0] + c2 * basis[1]
    left_over = right_side - (c0 * basis[0] + c1 * basis[1] + c2 * basis[2])
    return solved, left_over, skr[:, :count].T


def solution(mesh):
    in_specs = (P(None, "gx", "gy"), P("gx", "gy"), P(), P("gx", "gy"), P("gx", "gy"))
    out_specs = (P(None, "gx", "gy"), P(None, "gx", "gy"), P(None, ("gx", "gy")))
    fn = functools.partial(shards, mesh.shape["gx"], mesh.shape["gy"])
    return jax.shard_map(fn, mesh=mesh, in_specs=in_specs, out_specs=out_specs, check_vma=False)
```

```python
import functools

import jax
import jax.numpy as jnp
from jax import lax
from jax.experimental import pallas as pl
from jax.experimental.pallas import tpu as pltpu
from jax.sharding import PartitionSpec as P

MESH = pl.DeviceIdType.MESH
DIAG = 2.4
RIDGE = 1e-05
HALO = 3
UNROLL = 14
PIECES = 4


def kernel(
    ngx, ngy, rows, cols, width,
    x_ref, ab_ref, tiles_ref, index_ref, sign_ref,
    basis_ref, y_ref, skr_ref,
    v0, v1, v2, v3, inv, tl, packs, got, abh, fold, sk, part1, mid, part2, gath, gath1, gath2,
    w_ref,
    in_sem, out_sem, row_send, row_recv, col_send, col_recv, ab_send, ab_recv,
    s1s, s1r, s2s, s2r, g1s, g1r, g2s, g2r,
):
    gx = lax.axis_index("gx")
    gy = lax.axis_index("gy")
    ext = rows + 2 * HALO
    wide = cols + 128

    x_copy = pltpu.make_async_copy(x_ref, v0.at[HALO:HALO + rows, 0:32, 0:cols], in_sem.at[0])
    for r in range(rows):
        pltpu.make_async_copy(x_ref.at[:, r, :], v0.at[HALO + r, 0:32, 0:cols], in_sem.at[0]).start()
    t_copy = pltpu.make_async_copy(tiles_ref, tl, in_sem.at[1])
    t_copy.start()

    barrier = pltpu.get_barrier_semaphore()
    for k in range(1, ngx):
        pl.semaphore_signal(barrier, inc=1, device_id=(lax.rem(gx + k, ngx), gy), device_id_type=MESH)
    for k in range(1, ngy):
        pl.semaphore_signal(barrier, inc=1, device_id=(gx, lax.rem(gy + k, ngy)), device_id_type=MESH)
    up, down = gx > 0, gx < ngx - 1
    left, right = gy > 0, gy < ngy - 1
    there = {-1: up, 0: None, 1: down}
    side_there = (left, right)

    def both(a, b):
        return b if a is None else jnp.logical_and(a, b)

    for dx in (-1, 1):
        for side, dy in enumerate((-1, 1)):
            @pl.when(both(there[dx], side_there[side]))
            def _(dx=dx, dy=dy):
                pl.semaphore_signal(barrier, inc=1, device_id=(gx + dx, gy + dy), device_id_type=MESH)
    n_v = up.astype(jnp.int32) + down.astype(jnp.int32)
    n_h = left.astype(jnp.int32) + right.astype(jnp.int32)

    for r in range(ext):
        if HALO <= r < HALO + rows:
            sign = (2 * sign_ref[r - HALO] - 1).astype(jnp.float32)
            for k in range(2):
                w_ref[k, r] = jnp.where(index_ref[r - HALO] == k, sign, 0.0)
        else:
            w_ref[0, r] = 0.0
            w_ref[1, r] = 0.0

    for r in range(rows):
        v0[HALO + r, 32:40, 0:cols] = jnp.broadcast_to(ab_ref[r:r + 1, :], (8, cols))
    x_copy.wait()

    lane = lax.broadcasted_iota(jnp.int32, (40, 128), 1)

    def pack(r, acc):
        here = (lane >= 4 * r) & (lane < 4 * r + 4)
        first = pltpu.roll(v0[HALO + r, :, 0:128], 4 * r, 1)
        last = pltpu.roll(v0[HALO + r, :, cols - 128:cols], lax.rem(4 * r + 4, 128), 1)
        return jnp.where(here, first, acc[0]), jnp.where(here, last, acc[1])

    zero = jnp.zeros((40, 128), jnp.float32)
    first, last = lax.fori_loop(0, rows, pack, (zero, zero))
    packs[0] = first
    packs[1] = last

    pl.semaphore_wait(barrier, ngx - 1 + ngy - 1 + n_v * n_h)

    row_copies = []
    for d, (dx, here) in enumerate(((-1, up), (1, down))):
        src = HALO if dx < 0 else rows
        dst = HALO + rows if dx < 0 else 0
        row_copies.append((pltpu.make_async_remote_copy(
            src_ref=v0.at[src:src + HALO, 0:32, 0:cols], dst_ref=v0.at[dst:dst + HALO, 0:32, 0:cols],
            send_sem=row_send.at[d], recv_sem=row_recv.at[d],
            device_id=(gx + dx, gy), device_id_type=MESH), here, (down, up)[d]))
        ar = 0 if dx < 0 else rows - 8
        row_copies.append((pltpu.make_async_remote_copy(
            src_ref=ab_ref.at[ar:ar + 8, :], dst_ref=abh.at[d],
            send_sem=ab_send.at[d], recv_sem=ab_recv.at[d],
            device_id=(gx + dx, gy), device_id_type=MESH), here, (down, up)[d]))
    col_copies = []
    for side, dy in enumerate((-1, 1)):
        for i, dx in enumerate((0, -1, 1)):
            slot = side * 3 + i
            to = both(there[dx], side_there[side])
            frm = both(there[-dx], side_there[1 - side])
            col_copies.append((pltpu.make_async_remote_copy(
                src_ref=packs.at[side], dst_ref=got.at[slot],
                send_sem=col_send.at[slot], recv_sem=col_recv.at[slot],
                device_id=(gx + dx, gy + dy), device_id_type=MESH), to, frm))
    for copy, to, frm in col_copies + row_copies:
        @pl.when(to)
        def _(copy=copy):
            copy.start()

    for d, frm in enumerate((down, up)):
        dst = HALO + rows if d == 0 else 0
        @pl.when(jnp.logical_not(frm))
        def _(d=d, dst=dst):
            v0[dst:dst + HALO, 0:32, 0:cols] = jnp.zeros((HALO, 32, cols), jnp.float32)
            abh[d] = jnp.zeros((8, cols), jnp.float32)
    for slot, (copy, to, frm) in enumerate(col_copies):
        @pl.when(jnp.logical_not(frm))
        def _(slot=slot):
            got[slot] = jnp.zeros((40, 128), jnp.float32)

    z = jnp.zeros((8, cols), jnp.float32)
    for t in range(4):
        q0 = slice(8 * t, 8 * t + 8)

        def fold_rows(r, acc, q0=q0):
            a0, a1 = acc
            for u in range(4):
                o = v0[r * 4 + u + HALO, q0, 0:cols]
                a0 = a0 + w_ref[0, r * 4 + u + HALO] * o
                a1 = a1 + w_ref[1, r * 4 + u + HALO] * o
            return a0, a1

        a0, a1 = lax.fori_loop(0, rows // 4, fold_rows, (z, z))
        fold[0, q0, :] = a0
        fold[1, q0, :] = a1

    def wait_recv(copies):
        for copy, to, frm in copies:
            @pl.when(frm)
            def _(copy=copy):
                copy.wait_recv()

    wait_recv([col_copies[0], col_copies[3]])

    def unpack(slot_right, slot_left, r, dest):
        a = pltpu.roll(got[slot_right], lax.rem(128 - 4 * r, 128), 1)
        b = pltpu.roll(got[slot_left], lax.rem(252 - 4 * r, 128), 1)
        v0[dest, :, cols:wide] = jnp.where(lane < 4, a, jnp.where(lane >= 124, b, 0.0))

    lane_w = lax.broadcasted_iota(jnp.int32, (8, wide), 1)
    col_in = (lane_w < cols) | ((lane_w < cols + HALO) & right) | ((lane_w >= wide - HALO) & left)

    def make_inv(r):
        row = gx * rows + r - HALO
        ok = col_in & (row >= 0) & (row < rows * ngx)
        inv[r] = jnp.where(ok, 1.0 / (DIAG + v0[r, 32:40, :]), 0.0)

    def unpack_own(r, c):
        for u in range(4):
            unpack(0, 3, 4 * r + u, HALO + 4 * r + u)
        for u in range(4):
            make_inv(HALO + 4 * r + u)
        return c

    lax.fori_loop(0, rows // 4, unpack_own, 0)

    def step(src, dst, n, lo, hi, unroll, fresh):
        for t in range(4):
            q = slice(8 * t, 8 * t + 8)

            def parts(r):
                v = src[r, q, :]
                e = pltpu.roll(v, wide - 1, 1)
                w = pltpu.roll(v, 1, 1)
                return v, e + w, e - w

            vp, _, dp = parts(lo - 1)
            up0 = 0.2 * vp + 0.15 * dp

            def row(r, carry):
                upv, v, s, d, a0, a1 = carry
                vn, sn, dn = parts(r + 1)
                out = v - inv[r] * (s + upv + (0.2 * vn - 0.15 * dn))
                dst[r, q, :] = out
                o = out[:, 0:cols]
                a0 = a0 + w_ref[0, r] * o
                a1 = a1 + w_ref[1, r] * o
                return 0.2 * v + 0.15 * d, vn, sn, dn, a0, a1

            def body(i, carry):
                for u in range(unroll):
                    carry = row(lo + i * unroll + u, carry)
                return carry

            v, s, d = parts(lo)
            fq = slice(32 * n + 8 * t, 32 * n + 8 * t + 8)
            start = (z, z) if fresh else (fold[0, fq, :], fold[1, fq, :])
            carry = (up0, v, s, d) + start
            trips = (hi - lo) // unroll
            if trips > 1:
                carry = lax.fori_loop(0, trips, body, carry)
            else:
                carry = body(0, carry)
            for r in range(lo + trips * unroll, hi):
                carry = row(r, carry)
            fold[0, fq, :] = carry[4]
            fold[1, fq, :] = carry[5]

    for n, (src, dst) in enumerate(((v0, v1), (v1, v2), (v2, v3)), 1):
        step(src, dst, n, HALO + n, ext - HALO - n, UNROLL, True)

    wait_recv(col_copies[1:3] + col_copies[4:] + row_copies)
    for i in range(HALO):
        v0[i, 32:40, 0:cols] = jnp.broadcast_to(abh[1, 8 - HALO + i:8 - HALO + i + 1, :], (8, cols))
        v0[HALO + rows + i, 32:40, 0:cols] = jnp.broadcast_to(abh[0, i:i + 1, :], (8, cols))
        unpack(1, 4, i, HALO + rows + i)
        unpack(2, 5, rows - HALO + i, i)
    for i in range(HALO):
        make_inv(i)
        make_inv(HALO + rows + i)
    for n, (src, dst) in enumerate(((v0, v1), (v1, v2), (v2, v3)), 1):
        step(src, dst, n, n, HALO + n, HALO, False)
        step(src, dst, n, ext - HALO - n, ext - n, HALO, False)
    out_copies = []
    for n, v in enumerate((v1, v2, v3)):
        for r in range(rows):
            pltpu.make_async_copy(v.at[HALO + r, :, 0:cols], basis_ref.at[n, :, r, :], out_sem.at[n]).start()
        out_copies.append(pltpu.make_async_copy(v.at[HALO:HALO + rows, :, 0:cols], basis_ref.at[n], out_sem.at[n]))
    t_copy.wait()

    block = ngy * width

    def halves(a):
        hi = a.astype(jnp.bfloat16)
        return hi, (a - hi.astype(jnp.float32)).astype(jnp.bfloat16)

    fold_hi, fold_lo = zip(*[halves(fold[k]) for k in range(2)])

    def nt(a, b):
        return lax.dot_general(a, b, (((1,), (1,)), ((), ())), preferred_element_type=jnp.float32)

    def mm(g, c):
        rows_g = pl.ds(pl.multiple_of(g * block, block), block)
        out = jnp.zeros((block, 128), jnp.float32)
        for k in range(2):
            hi, lo = halves(tl[k, rows_g, :])
            out = out + (nt(hi, fold_hi[k]) + (nt(hi, fold_lo[k]) + nt(lo, fold_hi[k])))
        for j in range(ngy):
            sk[j, g] = out[j * width:(j + 1) * width, :]
        return c

    def exchange(n, axis, pick, land, ss, rs):
        me = gx if axis == 0 else gy
        out = []
        for k in range(1, n):
            peer = lax.rem(me + k, n)
            out.append(pltpu.make_async_remote_copy(
                src_ref=pick(peer), dst_ref=land.at[k - 1], send_sem=ss.at[k - 1], recv_sem=rs.at[k - 1],
                device_id=(peer, gy) if axis == 0 else (gx, peer), device_id_type=MESH))
        for c in out:
            c.start()
        return out

    pieces = min(PIECES, ngx)
    span = ngx // pieces
    c1 = []
    for b in range(pieces):
        lax.fori_loop(b * span, (b + 1) * span, mm, 0)
        part = slice(b * span, (b + 1) * span)
        sends = []
        for k in range(1, ngy):
            peer = lax.rem(gy + k, ngy)
            sends.append(pltpu.make_async_remote_copy(
                src_ref=sk.at[peer, part], dst_ref=part1.at[k - 1, part],
                send_sem=s1s.at[k - 1, b], recv_sem=s1r.at[k - 1, b],
                device_id=(gx, peer), device_id_type=MESH))
        for c in sends:
            c.start()
        c1.append(sends)

    def to_owner(p, land):
        return pltpu.make_async_remote_copy(
            src_ref=mid.at[p], dst_ref=part2.at[land], send_sem=s2s.at[p], recv_sem=s2r.at[land],
            device_id=(p, gy), device_id_type=MESH)

    for b in range(pieces):
        part = slice(b * span, (b + 1) * span)
        total = sk[gy, part]
        for k, c in enumerate(c1[b]):
            c.wait_recv()
            total = total + part1[k, part]
        mid[part] = total
        for p in range(b * span, (b + 1) * span):
            @pl.when(p != gx)
            def _(p=p):
                to_owner(p, gx).start()
    part2[gx] = mid[gx]
    for p in range(ngx):
        @pl.when(p != gx)
        def _(p=p):
            to_owner(p, p).wait_recv()
    own = part2[0]
    for p in range(1, ngx):
        own = own + part2[p]

    prods = [jnp.sum(own * own, 0, keepdims=True)]
    for k in (1, 2):
        prods.append(jnp.sum(own * pltpu.roll(own, 32 * k, 1), 0, keepdims=True))
    gath[0] = jnp.concatenate(prods + [jnp.zeros((5, 128), jnp.float32)], 0)
    c3 = exchange(ngy, 1, lambda p: gath.at[0], gath1, g1s, g1r)
    tot = gath[0]
    for k, c in enumerate(c3):
        c.wait_recv()
        tot = tot + gath1[k]
    gath[1] = tot
    c4 = exchange(ngx, 0, lambda p: gath.at[1], gath2, g2s, g2r)
    for k, c in enumerate(c4):
        c.wait_recv()
        tot = tot + gath2[k]

    by = [tot] + [pltpu.roll(tot, 128 - 32 * f, 1) for f in (1, 2, 3)]

    def at(k, f):
        return by[f][k:k + 1, :]

    g00, g11, g22 = at(0, 1), at(0, 2), at(0, 3)
    g10, g21, g20 = at(1, 2), at(1, 3), at(2, 3)
    h0, h1, h2 = at(1, 1), at(2, 2), at(1, 0)
    ridge = RIDGE * (g00 + g11 + g22)
    p0 = jnp.sqrt(g00 + ridge)
    l10 = g10 / p0
    l20 = g20 / p0
    p1 = jnp.sqrt(g11 + ridge - l10 * l10)
    l21 = (g21 - l20 * l10) / p1
    p2 = jnp.sqrt(g22 + ridge - l20 * l20 - l21 * l21)
    f0 = h0 / p0
    f1 = (h1 - l10 * f0) / p1
    f2 = (h2 - l20 * f0 - l21 * f1) / p2
    y2 = f2 / p2
    y1 = (f1 - l21 * y2) / p1
    y0 = (f0 - l10 * y1 - l20 * y2) / p0

    rest = own - (y0 * pltpu.roll(own, 96, 1) + y1 * pltpu.roll(own, 64, 1) + y2 * pltpu.roll(own, 32, 1))
    skr_ref[...] = rest.T[0:32, :]

    y_ref[...] = jnp.concatenate([y0, y1, y2, jnp.zeros((5, 128), jnp.float32)], 0)

    for copy, to, frm in col_copies + row_copies:
        @pl.when(to)
        def _(copy=copy):
            copy.wait_send()
    for c in sum(c1, []) + c3 + c4:
        c.wait_send()
    for p in range(ngx):
        @pl.when(p != gx)
        def _(p=p):
            to_owner(p, p).wait_send()
    for oc in out_copies:
        oc.wait()


def shards(ngx, ngy, right_side, absorb, tiles, tile_index, tile_sign):
    count, rows, cols = right_side.shape
    sketch = tiles.shape[1]
    width = sketch // (ngx * ngy)
    ext, wide = rows + 2 * HALO, cols + 128
    f32 = jnp.float32
    dma = pltpu.SemaphoreType.DMA
    any_spec = pl.BlockSpec(memory_space=pl.ANY)
    vmem_spec = pl.BlockSpec(memory_space=pltpu.VMEM)
    basis, y, skr = pl.pallas_call(
        functools.partial(kernel, ngx, ngy, rows, cols, width),
        out_shape=(
            jax.ShapeDtypeStruct((3, count, rows, cols), f32),
            jax.ShapeDtypeStruct((8, 128), f32),
            jax.ShapeDtypeStruct((count, width), f32),
        ),
        in_specs=[any_spec, vmem_spec, any_spec] + [pl.BlockSpec(memory_space=pltpu.SMEM)] * 2,
        out_specs=(any_spec, vmem_spec, vmem_spec),
        scratch_shapes=[
            pltpu.VMEM((ext, 40, wide), f32),
            pltpu.VMEM((ext, 32, wide), f32),
            pltpu.VMEM((ext, 32, wide), f32),
            pltpu.VMEM((ext, 32, wide), f32),
            pltpu.VMEM((ext, 8, wide), f32),
            pltpu.VMEM(tiles.shape, f32),
            pltpu.VMEM((2, 40, 128), f32),
            pltpu.VMEM((6, 40, 128), f32),
            pltpu.VMEM((2, 8, cols), f32),
            pltpu.VMEM((2, 128, cols), f32),
            pltpu.VMEM((ngy, ngx, width, 128), f32),
            pltpu.VMEM((ngy - 1, ngx, width, 128), f32),
            pltpu.VMEM((ngx, width, 128), f32),
            pltpu.VMEM((ngx, width, 128), f32),
            pltpu.VMEM((2, 8, 128), f32),
            pltpu.VMEM((ngy - 1, 8, 128), f32),
            pltpu.VMEM((ngx - 1, 8, 128), f32),
            pltpu.SMEM((2, ext), f32),
            dma((2,)), dma((3,)), dma((2,)), dma((2,)), dma((6,)), dma((6,)), dma((2,)), dma((2,)),
            dma((ngy - 1, PIECES)), dma((ngy - 1, PIECES)), dma((ngx,)), dma((ngx,)),
            dma((ngy - 1,)), dma((ngy - 1,)), dma((ngx - 1,)), dma((ngx - 1,)),
        ],
        compiler_params=pltpu.CompilerParams(
            collective_id=0, has_side_effects=True, vmem_limit_bytes=56 * 2**20
        ),
    )(right_side, absorb, tiles, tile_index[:, 0], tile_sign[:, 0])
    c0, c1, c2 = [y[k, :count, None, None] for k in range(3)]
    solved = c0 * right_side + c1 * basis[0] + c2 * basis[1]
    left_over = right_side - (c0 * basis[0] + c1 * basis[1] + c2 * basis[2])
    return solved, left_over, skr


def solution(mesh):
    in_specs = (P(None, "gx", "gy"), P("gx", "gy"), P(), P("gx", "gy"), P("gx", "gy"))
    out_specs = (P(None, "gx", "gy"), P(None, "gx", "gy"), P(None, ("gx", "gy")))
    fn = functools.partial(shards, mesh.shape["gx"], mesh.shape["gy"])
    return jax.shard_map(fn, mesh=mesh, in_specs=in_specs, out_specs=out_specs, check_vma=False)
```
